32 devices in a mesh: interval: 4 (over y, x), slab: 8 (over z, core).
Axes of the slice: x: 2, y: 2, z: 4, core: 2. Of those that a mesh axis runs over, the one named last changes fastest.
Arguments:
- states: float32 [8, 16, 256, 512], P('interval', 'slab'), may hold values from -0.9 to 0.9
- occupations: int32 [8], P('interval'), may hold values from 1 to 64
- core_density: float32 [16, 256, 512], P('slab'), may hold values from 0.1 to 1
Outputs:
- potential: float32 [16, 256, 512], P('slab', 'interval')
The draws below stay inside these ranges and needn't reach their ends.
All inputs are finite; a program needn't handle non-finite values.
Results may differ from the reference program's by a relative error of at most 0.00002.
Values sent between devices are 32-bit elements; how exact they have to be, the bound alone decides.
A program may use at most 64 MiB of HBM per device.

```python
import math
import jax
import jax.numpy as jnp
from jax import lax

NX = 256
NY = 512
NZ = 16
NSTATES = 8


def set_ends(array, stream_key, smallest, top_value):
    index_at = [jax.random.randint(jax.random.fold_in(stream_key, axis), (), 0, length) for axis, length in enumerate(array.shape)]
    longest = array.shape.index(max(array.shape))
    neighbour = index_at[:longest] + [(index_at[longest] + 1) % array.shape[longest]] + index_at[longest + 1:]
    return array.at[tuple(index_at)].set(smallest).at[tuple(neighbour)].set(top_value)


def levels(stream_key, shape, split, smallest, high):
    def one(dim, parts):
        draws = jax.random.uniform(jax.random.fold_in(jax.random.fold_in(stream_key, 6), dim), (parts,), jnp.float32, smallest / len(split), high / len(split))
        return jnp.repeat(jnp.exp(draws), shape[dim] // parts).reshape((-1,) + (1,) * (len(shape) - dim - 1))

    loudness = one(*split[0])
    for cut in split[1:]:
        loudness = loudness * one(*cut)
    return loudness


def normal_values(stream_key, dims, deviation, reach, cuts=(), kind=jnp.bfloat16):
    values = deviation * jax.random.normal(stream_key, dims, jnp.float32)
    if cuts:
        values = values * levels(stream_key, dims, cuts, -0.22, 0.18)
    return jnp.clip(values, -reach, reach).astype(kind)


def setup_inputs(seed: int = 0) -> dict:
    seeds = jax.random.split(jax.random.key(seed), 4)
    states = normal_values(seeds[0], (NSTATES, NZ, NX, NY), 0.15, 0.9, ((0, 4), (1, 8)), jnp.float32)
    occupations = set_ends(jax.random.randint(seeds[1], (NSTATES,), 1, 65), jax.random.fold_in(seeds[1], 1), 1, 64).astype(jnp.int32)
    core_density = jnp.clip(jnp.exp(math.log(1.0) - 2.3025851 * jax.random.uniform(seeds[2], (NZ, NX, NY), jnp.float32) ** levels(seeds[2], (NZ, NX, NY), ((0, 8),), -0.2, 0.2)), 0.1, 1.0)
    return {"states": states, "occupations": occupations, "core_density": core_density}


spacing = 0.25
denominator = 64.0
pbe_kappa = 0.804
pbe_mu = 0.2195149727645171
pbe_beta = 0.06672455060314922
pw_alpha = 0.0310907

def deriv_roll(field, axis):
    near = jnp.roll(field, -1, axis) - jnp.roll(field, 1, axis)
    far = jnp.roll(field, -2, axis) - jnp.roll(field, 2, axis)
    return (8.0 * near - far) / (12.0 * spacing)

def pbe_energy(density, grad_sq):
    pbe_gamma = (1.0 - jnp.log(2.0)) / jnp.pi ** 2
    k_fermi = jnp.cbrt(3.0 * jnp.pi ** 2 * density)
    ex_unif = -0.75 * jnp.cbrt(3.0 / jnp.pi) * jnp.cbrt(density)
    s_sq = grad_sq / (4.0 * k_fermi ** 2 * density ** 2)
    f_exch = 1.0 + pbe_kappa - pbe_kappa / (1.0 + pbe_mu * s_sq / pbe_kappa)
    radius = jnp.cbrt(3.0 / (4.0 * jnp.pi * density))
    root_r = jnp.sqrt(radius)
    lower = 2.0 * pw_alpha * (7.5957 * root_r + 3.5876 * radius + 1.6382 * radius * root_r + 0.49294 * radius ** 2)
    e_corr = -2.0 * pw_alpha * (1.0 + 0.2137 * radius) * jnp.log(1.0 + 1.0 / lower)
    k_screen = jnp.sqrt(4.0 * k_fermi / jnp.pi)
    t_sq = grad_sq / (4.0 * k_screen ** 2 * density ** 2)
    factor = pbe_beta / pbe_gamma / jnp.expm1(-e_corr / pbe_gamma)
    ratio_t = (1.0 + factor * t_sq) / (1.0 + factor * t_sq + factor ** 2 * t_sq ** 2)
    h_term = pbe_gamma * jnp.log(1.0 + pbe_beta / pbe_gamma * t_sq * ratio_t)
    return density * (ex_unif * f_exch + e_corr + h_term)

def local_derivs(density, grad_sq):
    return jax.grad(lambda rho, grd: jnp.sum(pbe_energy(rho, grd)), argnums=(0, 1))(density, grad_sq)

def reference(states, occupations, core_density):
    weights = occupations.astype(jnp.float32) / denominator

    def accumulate(index, total):
        one_state = lax.dynamic_index_in_dim(states, index, 0, keepdims=False)
        return total + weights[index] * one_state * one_state
    valence = lax.fori_loop(0, states.shape[0], accumulate, jnp.zeros(states.shape[1:], jnp.float32))
    density = valence + core_density
    grad_z = deriv_roll(density, 0)
    grad_x = deriv_roll(density, 1)
    grad_y = deriv_roll(density, 2)
    grad_sq = grad_z * grad_z + grad_x * grad_x + grad_y * grad_y
    energy_rho, energy_grad = local_derivs(density, grad_sq)
    diverge = deriv_roll(2.0 * energy_grad * grad_z, 0) + deriv_roll(2.0 * energy_grad * grad_x, 1) + deriv_roll(2.0 * energy_grad * grad_y, 2)
    return energy_rho - diverge
```

```python
import functools
import math

import jax
import jax.numpy as jnp
from jax import lax
from jax.experimental import pallas as pl
from jax.experimental.pallas import tpu as pltpu
from jax.sharding import PartitionSpec as P

spacing = 0.25
denominator = 64.0
pbe_kappa = 0.804
pbe_mu = 0.2195149727645171
pbe_beta = 0.06672455060314922
pw_alpha = 0.0310907
pbe_gamma = (1.0 - math.log(2.0)) / math.pi**2
MESH = pl.DeviceIdType.MESH
edge = 8


def five_point(low2, low1, high1, high2):
    return (8.0 * (high1 - low1) - (high2 - low2)) * (1.0 / (12.0 * spacing))


def deriv_y(field):
    axis = field.ndim - 1
    count = field.shape[axis]
    return five_point(
        pltpu.roll(field, 2, axis),
        pltpu.roll(field, 1, axis),
        pltpu.roll(field, count - 1, axis),
        pltpu.roll(field, count - 2, axis),
    )


def deriv_x(tall):
    return five_point(
        tall[:, edge - 2 : -edge - 2],
        tall[:, edge - 1 : -edge - 1],
        tall[:, edge + 1 : 1 - edge],
        tall[:, edge + 2 : 2 - edge],
    )


def pbe_derivs(n, g):
    k_one = (3.0 * math.pi**2) ** (1.0 / 3.0)
    ex_one = -0.75 * (3.0 / math.pi) ** (1.0 / 3.0)
    r_one = (3.0 / (4.0 * math.pi)) ** (1.0 / 3.0)
    s_one = 1.0 / (4.0 * k_one**2)
    t_one = math.pi / (16.0 * k_one)
    ratio = pbe_beta / pbe_gamma
    inv_six = jnp.exp(jnp.log(n) * (-1.0 / 6.0))
    inv = inv_six * inv_six
    inv2 = inv * inv
    inv4 = inv2 * inv2
    cube = n * inv2
    s_sq = (s_one * g) * (inv4 * inv4)
    u_inv = 1.0 / (1.0 + (pbe_mu / pbe_kappa) * s_sq)
    f_exch = (1.0 + pbe_kappa) - pbe_kappa * u_inv
    f_slope = pbe_mu * u_inv * u_inv
    ex_rho = (ex_one * cube) * ((4.0 / 3.0) * f_exch - (8.0 / 3.0) * f_slope * s_sq)

    radius = r_one * inv
    root = math.sqrt(r_one) * inv_six
    two_a = 2.0 * pw_alpha
    lower = (two_a * root) * (
        7.5957 + root * (3.5876 + root * (1.6382 + root * 0.49294))
    )
    slope = (two_a * root) * (
        0.5 * 7.5957 + root * (3.5876 + root * (1.5 * 1.6382 + root * (2.0 * 0.49294)))
    )
    pair_inv = 1.0 / (lower * (lower + 1.0))
    log_term = jnp.log(1.0 + (lower + 1.0) * pair_inv)
    front = two_a + (two_a * 0.2137) * radius
    e_corr = -front * log_term
    n_ec = (1.0 / 3.0) * ((two_a * 0.2137) * radius * log_term - front * slope * pair_inv)

    grown = jnp.exp(e_corr * (-1.0 / pbe_gamma))
    factor = ratio / (grown - 1.0)
    t_sq = (t_one * g) * (inv4 * inv2 * inv)
    y = factor * t_sq
    lift = 1.0 + y
    den = lift + y * y
    add = (ratio * t_sq) * lift
    full = den + add
    inv_full = 1.0 / (den * full)
    h_term = pbe_gamma * jnp.log(1.0 + add * (full * inv_full))
    h_t = (pbe_beta * inv_full) * (1.0 + 2.0 * y)
    h_ec = -(y * y) * (y * (2.0 + y)) * inv_full * grown
    e_rho = ex_rho + e_corr + h_term + n_ec + h_ec * n_ec - (7.0 / 3.0) * (t_sq * h_t)
    e_grad = inv4 * (t_one * h_t + (ex_one * s_one) * f_slope)
    return e_rho, e_grad


def plan(chunks, square):
    order = []
    for i in range((chunks + 1) // 2):
        order += [i] if i == chunks - 1 - i else [i, chunks - 1 - i]
    twin = set(range(1, chunks - 1))
    steps = [("send", c) for c in order] + [("gather", c) for c in order]
    steps += [("edges", 0)] + [("energy", c) for c in order if c not in twin]
    steps += [("energy", c) for c in order if c in twin]
    steps += [("edges", 1)] + [("diverge", c) for c in order]
    return steps, set(order), twin


def kernel(
    peers, slabs, rows, steps, direct, twin,
    states, occ, core, out,
    stage, core_v, snd, rcv, pair_out, pair_in, pass_out, pass_in, dens, fz, fx, rim_out, rim_in,
    in_sem, core_sem, rs_send, rs_recv, pair_send, pair_recv, pass_send, pass_recv,
    z_send, z_recv, f_send, f_recv, x_send, x_recv,
):
    nst, nz, wide = stage.shape[1], stage.shape[2], stage.shape[3]
    chunks = wide // rows
    me = lax.axis_index("interval")
    sl = lax.axis_index("slab")
    odd = lax.rem(sl, 2)
    way = 1 - 2 * odd

    def slab(step):
        return lax.rem(sl + step * way + slabs, slabs)

    sib, near_z, far_z, far_back = slab(1), slab(-1), slab(2), slab(-2)
    x_low = lax.rem(me + peers - 1, peers)
    x_high = lax.rem(me + 1, peers)
    square = peers == 4
    if square:
        hi, lo = lax.div(me, 2), lax.rem(me, 2)
        peer = [me, me + 1 - 2 * lo, me + 2 - 4 * hi, 3 - me]
    else:
        peer = [lax.rem(me + k, peers) for k in range(peers)]

    barrier = pltpu.get_barrier_semaphore()
    for k in range(1, peers):
        pl.semaphore_signal(
            barrier, inc=1, device_id=(peer[k], sl), device_id_type=MESH
        )
    greeted = [sib, near_z] + ([far_z, far_back] if twin else [])
    for z in greeted:
        pl.semaphore_signal(barrier, inc=1, device_id=(me, z), device_id_type=MESH)

    def pull(k):
        start = pl.multiple_of(peer[k] * wide, 8)
        return pltpu.make_async_copy(
            states.at[:, :, pl.ds(start, wide), :], stage.at[k], in_sem.at[k]
        )

    for k in [*range(1, peers), 0]:
        pull(k).start()
    core_copy = pltpu.make_async_copy(
        core.at[:, pl.ds(pl.multiple_of(me * wide, 8), wide), :], core_v, core_sem
    )
    core_copy.start()

    weights = [occ[s].astype(jnp.float32) * (1.0 / denominator) for s in range(nst)]

    def term(k, p, at):
        total = None
        for s in range(nst):
            value = stage[k, s, p, pl.ds(at, rows), :]
            part = (weights[s] * value) * value
            total = part if total is None else total + part
        return total

    def remote(source, target, sems, device):
        return pltpu.make_async_remote_copy(
            src_ref=source,
            dst_ref=target,
            send_sem=sems[0],
            recv_sem=sems[1],
            device_id=device,
            device_id_type=MESH,
        )

    def share(c, k):
        sems = rs_send.at[k - 1, c], rs_recv.at[k - 1, c]
        return remote(snd.at[c, k - 1], rcv.at[c, k - 1], sems, (peer[k], sl))

    def pair(c, p):
        sems = pair_send.at[p, c], pair_recv.at[p, c]
        return remote(pair_out.at[c, p], pair_in.at[c, p], sems, (peer[1 + p % 2], sl))

    def passed(c, p):
        sems = pass_send.at[p, c], pass_recv.at[p, c]
        return remote(pass_out.at[c, p], pass_in.at[c, p], sems, (peer[2 - p % 2], sl))

    def planes(c, k):
        span = pl.ds(edge + c * rows, rows)
        step = (1, -1, 2)[k]
        source = dens.at[pl.ds(2 * nz, nz), span, :]
        target = dens.at[pl.ds((2 - step * way) * nz, nz), span, :]
        sems = z_send.at[k, c], z_recv.at[k, c]
        return remote(source, target, sems, (me, (sib, near_z, far_z)[k]))

    def fluxes(c, k):
        span = pl.ds(c * rows, rows)
        step = (1, -1)[k]
        source = fz.at[pl.ds(nz, nz), span, :]
        target = fz.at[pl.ds((1 - step * way) * nz, nz), span, :]
        sems = f_send.at[k, c], f_recv.at[k, c]
        return remote(source, target, sems, (me, (sib, near_z)[k]))

    def sides(field, side):
        sems = x_send.at[field, side], x_recv.at[field, side]
        return remote(
            rim_out.at[field, side], rim_in.at[field, side], sems, ((x_low, x_high)[side], sl)
        )

    started, waited = [], set()

    def start(copy):
        copy.start()
        started.append(copy)

    def arrived(name, make, *where):
        if (name, where) not in waited:
            waited.add((name, where))
            make(*where).wait_recv()

    def send(c):
        if c in direct:
            for k in (range(peers - 1, 0, -1)):
                if c == steps[0][1]:
                    pull(k).wait()
                for p in range(nz):
                    snd[c, k - 1, p] = term(k, p, c * rows)
        else:
            if c == steps[0][1]:
                for k in range(1, peers):
                    pull(k).wait()
            for p in range(nz):
                pair_out[c, p, 0] = term(1 + p % 2, p, c * rows)
                pair_out[c, p, 1] = term(3, p, c * rows)
        if c == steps[0][1]:
            pl.semaphore_wait(barrier, peers - 1 + len(greeted))
        if c in direct:
            for k in range(peers - 1, 0, -1):
                start(share(c, k))
        else:
            for p in range(nz):
                start(pair(c, p))

    def relay(c):
        for p in range(nz):
            arrived("pair", pair, c, p)
            pass_out[c, p] = term(2 - p % 2, p, c * rows) + pair_in[c, p, 1]
            start(passed(c, p))

    def gather(c):
        at = c * rows
        if c == order[0]:
            pull(0).wait()
            core_copy.wait()
        if c in direct:
            for k in range(1, peers):
                arrived("share", share, c, k)
        else:
            for p in range(nz):
                arrived("passed", passed, c, p)
        for p in range(nz):
            total = term(0, p, at) + core_v[p, pl.ds(at, rows), :]
            if c in direct:
                for k in range(1, peers):
                    total = total + rcv[c, k - 1, p]
            else:
                total = total + pair_in[c, p, 0] + pass_in[c, p]
            dens[2 * nz + p, pl.ds(edge + at, rows), :] = total
            if c == 0:
                rim_out[0, 0, p] = total[:2]
            if c == chunks - 1:
                rim_out[0, 1, p] = total[rows - 2 :]
        if c == 0:
            start(sides(0, 0))
        if c == chunks - 1:
            start(sides(0, 1))
        start(planes(c, 1))
        if c in twin:
            start(planes(c, 2))
        start(planes(c, 0))

    def edges(field):
        ref, base = ((dens, 2 * nz), (fx, 0))[field]
        for side in (0, 1):
            arrived("sides", sides, field, side)
        for p in range(nz):
            ref[base + p, pl.ds(edge + wide, 2), :] = rim_in[field, 0, p]
            ref[base + p, pl.ds(edge - 2, 2), :] = rim_in[field, 1, p]

    def energy(c):
        arrived("planes", planes, c, 0)
        arrived("planes", planes, c, 1)
        at = c * rows
        inner = pl.ds(at + edge, rows)

        def fields(plane):
            n = dens[plane, inner, :]
            low2, low1 = dens[plane - 2, inner, :], dens[plane - 1, inner, :]
            high1, high2 = dens[plane + 1, inner, :], dens[plane + 2, inner, :]
            grad_z = five_point(low2, low1, high1, high2)
            grad_x = deriv_x(dens[pl.ds(plane, 1), pl.ds(at, rows + 2 * edge), :])[0]
            grad_y = deriv_y(n)
            g = grad_z * grad_z + grad_x * grad_x + grad_y * grad_y
            e_rho, e_grad = pbe_derivs(n, g)
            return e_rho, 2.0 * e_grad, grad_z, grad_x, grad_y

        for p in range(nz):
            e_rho, twice, grad_z, grad_x, grad_y = fields(2 * nz + p)
            fz[nz + p, pl.ds(at, rows), :] = twice * grad_z
            flux_x = twice * grad_x
            fx[p, inner, :] = flux_x
            if c == 0:
                rim_out[1, 0, p] = flux_x[:2]
            if c == chunks - 1:
                rim_out[1, 1, p] = flux_x[rows - 2 :]
            out[p, pl.ds(at, rows), :] = e_rho - deriv_y(twice * grad_y)
        if c == 0:
            start(sides(1, 0))
        if c == chunks - 1:
            start(sides(1, 1))
        if c not in twin:
            start(fluxes(c, 1))
        start(fluxes(c, 0))
        if c in twin:
            arrived("planes", planes, c, 2)
            for d in (c - 1, c + 1):
                arrived("planes", planes, d, 1)
            for p in range(nz):
                _, twice, grad_z, _, _ = fields((2 - way) * nz + p)
                fz[(1 - way) * nz + p, pl.ds(at, rows), :] = twice * grad_z

    def diverge(c):
        arrived("fluxes", fluxes, c, 0)
        if c not in twin:
            arrived("fluxes", fluxes, c, 1)
        at = c * rows
        span = pl.ds(at, rows)
        for p in range(nz):
            div_z = five_point(
                fz[nz + p - 2, span, :], fz[nz + p - 1, span, :], fz[nz + p + 1, span, :], fz[nz + p + 2, span, :]
            )
            div_x = deriv_x(fx[p : p + 1, pl.ds(at, rows + 2 * edge), :])[0]
            out[p, span, :] = out[p, span, :] - (div_z + div_x)

    order = [c for name, c in steps if name == "send"]
    act = dict(send=send, relay=relay, gather=gather, edges=edges, energy=energy, diverge=diverge)
    for name, c in steps:
        act[name](c)
    for copy in started:
        copy.wait_send()


def shards(peers, slabs, states, occupations, core_density):
    nst, nz, full, deep = states.shape
    wide = full // peers
    rows = edge
    chunks = wide // rows
    steps, direct, twin = plan(chunks, peers == 4)
    f32 = jnp.float32
    dma = pltpu.SemaphoreType.DMA
    return pl.pallas_call(
        functools.partial(kernel, peers, slabs, rows, steps, direct, twin),
        out_shape=pltpu.VMEM((nz, wide, deep), f32),
        in_specs=[
            pl.BlockSpec(memory_space=pl.ANY),
            pl.BlockSpec(memory_space=pltpu.SMEM),
            pl.BlockSpec(memory_space=pl.ANY),
        ],
        out_specs=pl.BlockSpec(memory_space=pltpu.VMEM),
        scratch_shapes=[
            pltpu.VMEM((peers, nst, nz, wide, deep), f32),
            pltpu.VMEM((nz, wide, deep), f32),
            pltpu.VMEM((chunks, peers - 1, nz, rows, deep), f32),
            pltpu.VMEM((chunks, peers - 1, nz, rows, deep), f32),
            pltpu.VMEM((chunks, nz, 2, rows, deep), f32),
            pltpu.VMEM((chunks, nz, 2, rows, deep), f32),
            pltpu.VMEM((chunks, nz, rows, deep), f32),
            pltpu.VMEM((chunks, nz, rows, deep), f32),
            pltpu.VMEM((5 * nz, wide + 2 * edge, deep), f32),
            pltpu.VMEM((3 * nz, wide, deep), f32),
            pltpu.VMEM((nz, wide + 2 * edge, deep), f32),
            pltpu.VMEM((2, 2, nz, 2, deep), f32),
            pltpu.VMEM((2, 2, nz, 2, deep), f32),
            dma((peers,)),
            dma,
            dma((peers - 1, chunks)),
            dma((peers - 1, chunks)),
            dma((nz, chunks)),
            dma((nz, chunks)),
            dma((nz, chunks)),
            dma((nz, chunks)),
            dma((3, chunks)),
            dma((3, chunks)),
            dma((2, chunks)),
            dma((2, chunks)),
            dma((2, 2)),
            dma((2, 2)),
        ],
        compiler_params=pltpu.CompilerParams(
            collective_id=0, has_side_effects=True, vmem_limit_bytes=67043328 - 1024 * 1024
        ),
    )(states, occupations, core_density)


def solution(mesh):
    return jax.shard_map(
        functools.partial(shards, mesh.shape["interval"], mesh.shape["slab"]),
        mesh=mesh,
        in_specs=(P("interval", "slab", None, None), P("interval"), P("slab", None, None)),
        out_specs=P("slab", "interval", None),
        check_vma=False,
    )
```

```python
import functools
import math

import jax
import jax.numpy as jnp
from jax import lax
from jax.experimental import pallas as pl
from jax.experimental.pallas import tpu as pltpu
from jax.sharding import PartitionSpec as P

spacing = 0.25
denominator = 64.0
pbe_kappa = 0.804
pbe_mu = 0.2195149727645171
pbe_beta = 0.06672455060314922
pw_alpha = 0.0310907
pbe_gamma = (1.0 - math.log(2.0)) / math.pi**2
MESH = pl.DeviceIdType.MESH
edge = 8


def five_point(low2, low1, high1, high2):
    return (8.0 * (high1 - low1) - (high2 - low2)) * (1.0 / (12.0 * spacing))


def deriv_y(field):
    axis = field.ndim - 1
    count = field.shape[axis]
    return five_point(
        pltpu.roll(field, 2, axis),
        pltpu.roll(field, 1, axis),
        pltpu.roll(field, count - 1, axis),
        pltpu.roll(field, count - 2, axis),
    )


def deriv_x(tall):
    return five_point(
        tall[:, edge - 2 : -edge - 2],
        tall[:, edge - 1 : -edge - 1],
        tall[:, edge + 1 : 1 - edge],
        tall[:, edge + 2 : 2 - edge],
    )


def pbe_derivs(n, g):
    k_one = (3.0 * math.pi**2) ** (1.0 / 3.0)
    ex_one = -0.75 * (3.0 / math.pi) ** (1.0 / 3.0)
    r_one = (3.0 / (4.0 * math.pi)) ** (1.0 / 3.0)
    s_one = 1.0 / (4.0 * k_one**2)
    t_one = math.pi / (16.0 * k_one)
    ratio = pbe_beta / pbe_gamma
    inv_six = jnp.exp(jnp.log(n) * (-1.0 / 6.0))
    inv = inv_six * inv_six
    inv2 = inv * inv
    inv4 = inv2 * inv2
    cube = n * inv2
    s_sq = (s_one * g) * (inv4 * inv4)
    u_inv = 1.0 / (1.0 + (pbe_mu / pbe_kappa) * s_sq)
    f_exch = (1.0 + pbe_kappa) - pbe_kappa * u_inv
    f_slope = pbe_mu * u_inv * u_inv
    ex_rho = (ex_one * cube) * ((4.0 / 3.0) * f_exch - (8.0 / 3.0) * f_slope * s_sq)

    radius = r_one * inv
    root = math.sqrt(r_one) * inv_six
    two_a = 2.0 * pw_alpha
    lower = (two_a * root) * (
        7.5957 + root * (3.5876 + root * (1.6382 + root * 0.49294))
    )
    slope = (two_a * root) * (
        0.5 * 7.5957 + root * (3.5876 + root * (1.5 * 1.6382 + root * (2.0 * 0.49294)))
    )
    pair_inv = 1.0 / (lower * (lower + 1.0))
    log_term = jnp.log(1.0 + (lower + 1.0) * pair_inv)
    front = two_a + (two_a * 0.2137) * radius
    e_corr = -front * log_term
    n_ec = (1.0 / 3.0) * ((two_a * 0.2137) * radius * log_term - front * slope * pair_inv)

    grown = jnp.exp(e_corr * (-1.0 / pbe_gamma))
    factor = ratio / (grown - 1.0)
    t_sq = (t_one * g) * (inv4 * inv2 * inv)
    y = factor * t_sq
    lift = 1.0 + y
    den = lift + y * y
    add = (ratio * t_sq) * lift
    full = den + add
    inv_full = 1.0 / (den * full)
    h_term = pbe_gamma * jnp.log(1.0 + add * (full * inv_full))
    h_t = (pbe_beta * inv_full) * (1.0 + 2.0 * y)
    h_ec = -(y * y) * (y * (2.0 + y)) * inv_full * grown
    e_rho = ex_rho + e_corr + h_term + n_ec + h_ec * n_ec - (7.0 / 3.0) * (t_sq * h_t)
    e_grad = inv4 * (t_one * h_t + (ex_one * s_one) * f_slope)
    return e_rho, e_grad


def plan(chunks, ahead=4, turn=5):
    order = []
    for i in range((chunks + 1) // 2):
        order += [i] if i == chunks - 1 - i else [i, chunks - 1 - i]
    fine = set()
    last = order[-1]
    calm = [c for c in order if abs(c - last) > 1]
    late = [c for c in order if abs(c - last) == 1]
    turn = min(turn, chunks)
    steps = [("send", c) for c in order[:ahead]]
    for i, c in enumerate(order):
        steps.append(("gather", c))
        steps += [("send", d) for d in order[ahead + i : ahead + i + 1]]
        steps += [("edges", 0)] if i == turn - 1 else []
    steps += [("energy", c) for c in calm + late]
    steps += [("beyond", c) for c in calm if 0 < c < chunks - 1]
    steps += [("outer", 0)] + [("beyond", c) for c in calm if c in (0, chunks - 1)]
    done = [c for c in calm if 0 < c < chunks - 1]
    steps += [("diverge", c) for c in done]
    steps += [("energy", last)] + [("beyond", c) for c in late + [last]]
    steps += [("edges", 1)] + [("diverge", c) for c in order if c not in done]
    return steps, fine


def kernel(
    peers, slabs, rows, steps, fine,
    states, occ, core, out,
    stage, core_v, snd, rcv, dens, fz, fx, rim_out, rim_in, rim_near,
    in_sem, core_sem, rs_send, rs_recv,
    z_send, z_recv, f_send, f_recv, x_send, x_recv, c_send, c_recv,
):
    nst, nz, wide = stage.shape[1], stage.shape[2], stage.shape[3]
    chunks = wide // rows
    me = lax.axis_index("interval")
    sl = lax.axis_index("slab")
    odd = lax.rem(sl, 2)
    way = 1 - 2 * odd

    def slab(step):
        return lax.rem(sl + step * way + slabs, slabs)

    sib, near_z, far_z, far_back = slab(1), slab(-1), slab(2), slab(-2)
    x_low = lax.rem(me + peers - 1, peers)
    x_high = lax.rem(me + 1, peers)
    square = peers == 4
    if square:
        hi, lo = lax.div(me, 2), lax.rem(me, 2)
        peer = [me, me + 1 - 2 * lo, me + 2 - 4 * hi, 3 - me]
    else:
        peer = [lax.rem(me + k, peers) for k in range(peers)]

    barrier = pltpu.get_barrier_semaphore()
    greeted = [sib, near_z, far_z, far_back]
    for z in greeted:
        pl.semaphore_signal(barrier, inc=1, device_id=(me, z), device_id_type=MESH)
    for k in range(1, peers):
        pl.semaphore_signal(
            barrier, inc=1, device_id=(peer[k], sl), device_id_type=MESH
        )

    def pull(k):
        start = pl.multiple_of(peer[k] * wide, 8)
        return pltpu.make_async_copy(
            states.at[:, :, pl.ds(start, wide), :], stage.at[k], in_sem.at[k]
        )

    for k in [*range(1, peers), 0]:
        pull(k).start()
    core_copy = pltpu.make_async_copy(
        core.at[:, pl.ds(pl.multiple_of(me * wide, 8), wide), :], core_v, core_sem
    )
    core_copy.start()

    weights = [occ[s].astype(jnp.float32) * (1.0 / denominator) for s in range(nst)]

    def term(k, p, at):
        total = None
        for s in range(nst):
            value = stage[k, s, p, pl.ds(at, rows), :]
            part = (weights[s] * value) * value
            total = part if total is None else total + part
        return total

    def remote(source, target, sems, device):
        return pltpu.make_async_remote_copy(
            src_ref=source,
            dst_ref=target,
            send_sem=sems[0],
            recv_sem=sems[1],
            device_id=device,
            device_id_type=MESH,
        )

    def parts(c):
        return [(p, 1) for p in range(nz)] if c in fine else [(0, nz)]

    def share(c, k, p, count):
        sems = rs_send.at[k - 1, c, p], rs_recv.at[k - 1, c, p]
        span = pl.ds(p, count)
        return remote(snd.at[c, k - 1, span], rcv.at[c, k - 1, span], sems, (peer[k], sl))

    def planes(c, k, p, count):
        span = pl.ds(edge + c * rows, rows)
        step = (1, -1, 2)[k]
        source = dens.at[pl.ds(2 * nz + p, count), span, :]
        target = dens.at[pl.ds((2 - step * way) * nz + p, count), span, :]
        sems = z_send.at[k, c, p], z_recv.at[k, c, p]
        return remote(source, target, sems, (me, (sib, near_z, far_z)[k]))

    def fluxes(c):
        span = pl.ds(c * rows, rows)
        source = fz.at[pl.ds(nz, nz), span, :]
        target = fz.at[pl.ds((1 - way) * nz, nz), span, :]
        return remote(source, target, (f_send.at[c], f_recv.at[c]), (me, sib))

    def corners():
        return remote(rim_in.at[0], rim_near, (c_send, c_recv), (me, near_z))

    def sides(field, side):
        sems = x_send.at[field, side], x_recv.at[field, side]
        return remote(
            rim_out.at[field, side], rim_in.at[field, side], sems, ((x_low, x_high)[side], sl)
        )

    started, waited = [], set()

    def start(copy):
        copy.start()
        started.append(copy)

    def arrived(name, make, *where):
        if (name, where) not in waited:
            waited.add((name, where))
            make(*where).wait_recv()

    def landed(c, k):
        for part in parts(c):
            arrived("planes", planes, c, k, *part)

    def send(c):
        for k in range(peers - 1, 0, -1):
            if c == order[0]:
                pull(k).wait()
            for p in range(nz):
                snd[c, k - 1, p] = term(k, p, c * rows)
        if c == order[0]:
            pl.semaphore_wait(barrier, peers - 1 + len(greeted))
        for part in parts(c):
            for k in range(peers - 1, 0, -1):
                start(share(c, k, *part))

    def gather(c):
        at = c * rows
        if c == order[0]:
            pull(0).wait()
            core_copy.wait()
        for p, count in parts(c):
            for k in range(1, peers):
                share(c, k, p, count).wait_recv()
            for q in range(p, p + count):
                total = term(0, q, at) + core_v[q, pl.ds(at, rows), :]
                for k in range(1, peers):
                    total = total + rcv[c, k - 1, q]
                dens[2 * nz + q, pl.ds(edge + at, rows), :] = total
                if c == 0:
                    rim_out[0, 0, q] = total[:2]
                if c == chunks - 1:
                    rim_out[0, 1, q] = total[rows - 2 :]
            if c == 0 and p + count == nz:
                start(sides(0, 0))
            if c == chunks - 1 and p + count == nz:
                start(sides(0, 1))
            for k in (2, 1, 0):
                start(planes(c, k, p, count))

    def edges(field):
        ref, base = ((dens, 2 * nz), (fx, 0))[field]
        for side in (0, 1):
            arrived("sides", sides, field, side)
        if field == 0:
            start(corners())
        for p in range(nz):
            ref[base + p, pl.ds(edge + wide, 2), :] = rim_in[field, 0, p]
            ref[base + p, pl.ds(edge - 2, 2), :] = rim_in[field, 1, p]

    def outer(_):
        corners().wait_recv()
        base = (2 - way) * nz
        for p in range(nz):
            dens[base + p, pl.ds(edge + wide, 2), :] = rim_near[0, p]
            dens[base + p, pl.ds(edge - 2, 2), :] = rim_near[1, p]

    def fields(plane, at):
        inner = pl.ds(at + edge, rows)
        n = dens[plane, inner, :]
        low2, low1 = dens[plane - 2, inner, :], dens[plane - 1, inner, :]
        high1, high2 = dens[plane + 1, inner, :], dens[plane + 2, inner, :]
        grad_z = five_point(low2, low1, high1, high2)
        grad_x = deriv_x(dens[pl.ds(plane, 1), pl.ds(at, rows + 2 * edge), :])[0]
        grad_y = deriv_y(n)
        g = grad_z * grad_z + grad_x * grad_x + grad_y * grad_y
        e_rho, e_grad = pbe_derivs(n, g)
        return e_rho, 2.0 * e_grad, grad_z, grad_x, grad_y

    def energy(c):
        landed(c, 0)
        landed(c, 1)
        at = c * rows
        for p in range(nz):
            e_rho, twice, grad_z, grad_x, grad_y = fields(2 * nz + p, at)
            fz[nz + p, pl.ds(at, rows), :] = twice * grad_z
            flux_x = twice * grad_x
            fx[p, pl.ds(at + edge, rows), :] = flux_x
            if c == 0:
                rim_out[1, 0, p] = flux_x[:2]
            if c == chunks - 1:
                rim_out[1, 1, p] = flux_x[rows - 2 :]
            out[p, pl.ds(at, rows), :] = e_rho - deriv_y(twice * grad_y)
        start(fluxes(c))
        if c == 0:
            start(sides(1, 0))
        if c == chunks - 1:
            start(sides(1, 1))

    def beyond(c):
        landed(c, 2)
        for d in range(max(c - 1, 0), min(c + 2, chunks)):
            landed(d, 1)
        at = c * rows
        for p in range(nz):
            _, twice, grad_z, _, _ = fields((2 - way) * nz + p, at)
            fz[(1 - way) * nz + p, pl.ds(at, rows), :] = twice * grad_z

    def diverge(c):
        fluxes(c).wait_recv()
        at = c * rows
        span = pl.ds(at, rows)
        for p in range(nz):
            div_z = five_point(
                fz[nz + p - 2, span, :], fz[nz + p - 1, span, :], fz[nz + p + 1, span, :], fz[nz + p + 2, span, :]
            )
            div_x = deriv_x(fx[p : p + 1, pl.ds(at, rows + 2 * edge), :])[0]
            out[p, span, :] = out[p, span, :] - (div_z + div_x)

    order = [c for name, c in steps if name == "send"]
    act = dict(send=send, gather=gather, edges=edges, outer=outer, energy=energy, beyond=beyond, diverge=diverge)
    for name, c in steps:
        act[name](c)
    for copy in started:
        copy.wait_send()


def shards(peers, slabs, states, occupations, core_density):
    nst, nz, full, deep = states.shape
    wide = full // peers
    rows = edge
    chunks = wide // rows
    steps, fine = plan(chunks)
    f32 = jnp.float32
    dma = pltpu.SemaphoreType.DMA
    return pl.pallas_call(
        functools.partial(kernel, peers, slabs, rows, steps, fine),
        out_shape=pltpu.VMEM((nz, wide, deep), f32),
        in_specs=[
            pl.BlockSpec(memory_space=pl.ANY),
            pl.BlockSpec(memory_space=pltpu.SMEM),
            pl.BlockSpec(memory_space=pl.ANY),
        ],
        out_specs=pl.BlockSpec(memory_space=pltpu.VMEM),
        scratch_shapes=[
            pltpu.VMEM((peers, nst, nz, wide, deep), f32),
            pltpu.VMEM((nz, wide, deep), f32),
            pltpu.VMEM((chunks, peers - 1, nz, rows, deep), f32),
            pltpu.VMEM((chunks, peers - 1, nz, rows, deep), f32),
            pltpu.VMEM((5 * nz, wide + 2 * edge, deep), f32),
            pltpu.VMEM((3 * nz, wide, deep), f32),
            pltpu.VMEM((nz, wide + 2 * edge, deep), f32),
            pltpu.VMEM((2, 2, nz, 2, deep), f32),
            pltpu.VMEM((2, 2, nz, 2, deep), f32),
            pltpu.VMEM((2, nz, 2, deep), f32),
            dma((peers,)),
            dma,
            dma((peers - 1, chunks, nz)),
            dma((peers - 1, chunks, nz)),
            dma((3, chunks, nz)),
            dma((3, chunks, nz)),
            dma((chunks,)),
            dma((chunks,)),
            dma((2, 2)),
            dma((2, 2)),
            dma,
            dma,
        ],
        compiler_params=pltpu.CompilerParams(
            collective_id=0, has_side_effects=True, vmem_limit_bytes=67043328 - 1024 * 1024
        ),
    )(states, occupations, core_density)


def solution(mesh):
    return jax.shard_map(
        functools.partial(shards, mesh.shape["interval"], mesh.shape["slab"]),
        mesh=mesh,
        in_specs=(P("interval", "slab", None, None), P("interval"), P("slab", None, None)),
        out_specs=P("slab", "interval", None),
        check_vma=False,
    )
```

```python
import functools
import math

import jax
import jax.numpy as jnp
from jax import lax
from jax.experimental import pallas as pl
from jax.experimental.pallas import tpu as pltpu
from jax.sharding import PartitionSpec as P

spacing = 0.25
denominator = 64.0
pbe_kappa = 0.804
pbe_mu = 0.2195149727645171
pbe_beta = 0.06672455060314922
pw_alpha = 0.0310907
pbe_gamma = (1.0 - math.log(2.0)) / math.pi**2
MESH = pl.DeviceIdType.MESH
edge = 8


def five_point(low2, low1, high1, high2):
    return (8.0 * (high1 - low1) - (high2 - low2)) * (1.0 / (12.0 * spacing))


def deriv_y(field):
    axis = field.ndim - 1
    count = field.shape[axis]
    return five_point(
        pltpu.roll(field, 2, axis),
        pltpu.roll(field, 1, axis),
        pltpu.roll(field, count - 1, axis),
        pltpu.roll(field, count - 2, axis),
    )


def deriv_x(tall):
    return five_point(
        tall[:, edge - 2 : -edge - 2],
        tall[:, edge - 1 : -edge - 1],
        tall[:, edge + 1 : 1 - edge],
        tall[:, edge + 2 : 2 - edge],
    )


def pbe_derivs(n, g):
    k_one = (3.0 * math.pi**2) ** (1.0 / 3.0)
    ex_one = -0.75 * (3.0 / math.pi) ** (1.0 / 3.0)
    r_one = (3.0 / (4.0 * math.pi)) ** (1.0 / 3.0)
    s_one = 1.0 / (4.0 * k_one**2)
    t_one = math.pi / (16.0 * k_one)
    ratio = pbe_beta / pbe_gamma
    inv_six = jnp.exp(jnp.log(n) * (-1.0 / 6.0))
    inv = inv_six * inv_six
    inv2 = inv * inv
    inv4 = inv2 * inv2
    cube = n * inv2
    s_sq = (s_one * g) * (inv4 * inv4)
    u_inv = 1.0 / (1.0 + (pbe_mu / pbe_kappa) * s_sq)
    f_exch = (1.0 + pbe_kappa) - pbe_kappa * u_inv
    f_slope = pbe_mu * u_inv * u_inv
    ex_rho = (ex_one * cube) * ((4.0 / 3.0) * f_exch - (8.0 / 3.0) * f_slope * s_sq)

    radius = r_one * inv
    root = math.sqrt(r_one) * inv_six
    two_a = 2.0 * pw_alpha
    lower = (two_a * root) * (
        7.5957 + root * (3.5876 + root * (1.6382 + root * 0.49294))
    )
    slope = (two_a * root) * (
        0.5 * 7.5957 + root * (3.5876 + root * (1.5 * 1.6382 + root * (2.0 * 0.49294)))
    )
    pair_inv = 1.0 / (lower * (lower + 1.0))
    log_term = jnp.log(1.0 + (lower + 1.0) * pair_inv)
    front = two_a + (two_a * 0.2137) * radius
    e_corr = -front * log_term
    n_ec = (1.0 / 3.0) * ((two_a * 0.2137) * radius * log_term - front * slope * pair_inv)

    grown = jnp.exp(e_corr * (-1.0 / pbe_gamma))
    factor = ratio / (grown - 1.0)
    t_sq = (t_one * g) * (inv4 * inv2 * inv)
    y = factor * t_sq
    lift = 1.0 + y
    den = lift + y * y
    add = (ratio * t_sq) * lift
    full = den + add
    inv_full = 1.0 / (den * full)
    h_term = pbe_gamma * jnp.log(1.0 + add * (full * inv_full))
    h_t = (pbe_beta * inv_full) * (1.0 + 2.0 * y)
    h_ec = -(y * y) * (y * (2.0 + y)) * inv_full * grown
    e_rho = ex_rho + e_corr + h_term + n_ec + h_ec * n_ec - (7.0 / 3.0) * (t_sq * h_t)
    e_grad = inv4 * (t_one * h_t + (ex_one * s_one) * f_slope)
    return e_rho, e_grad


def plan(chunks, ahead=4, turn=5):
    order = []
    for i in range((chunks + 1) // 2):
        order += [i] if i == chunks - 1 - i else [i, chunks - 1 - i]
    last = order[-1]
    calm = [c for c in order if abs(c - last) > 1]
    late = [c for c in order if abs(c - last) == 1]
    turn = min(turn, chunks)
    steps = [("send", c) for c in order[:ahead]]
    for i, c in enumerate(order):
        steps.append(("gather", c))
        steps += [("send", d) for d in order[ahead + i : ahead + i + 1]]
        steps += [("edges", 0)] if i == turn - 1 else []
    steps += [("energy", c) for c in calm + late]
    steps += [("beyond", c) for c in calm if 0 < c < chunks - 1]
    steps += [("outer", 0)] + [("beyond", c) for c in calm if c in (0, chunks - 1)]
    done = [c for c in calm if 0 < c < chunks - 1]
    steps += [("diverge", c) for c in done]
    steps += [("energy", last)] + [("beyond", c) for c in late + [last]]
    steps += [("edges", 1)] + [("diverge", c) for c in order if c not in done]
    return steps


def kernel(
    peers, slabs, rows, steps,
    states, occ, core, out,
    stage, core_v, snd, rcv, dens, fz, fx, rim_out, rim_in, rim_near,
    in_sem, core_sem, rs_send, rs_recv,
    z_send, z_recv, f_send, f_recv, x_send, x_recv, c_send, c_recv,
):
    nst, nz, wide = stage.shape[1], stage.shape[2], stage.shape[3]
    chunks = wide // rows
    me = lax.axis_index("interval")
    sl = lax.axis_index("slab")
    odd = lax.rem(sl, 2)
    way = 1 - 2 * odd

    def slab(step):
        return lax.rem(sl + step * way + slabs, slabs)

    sib, near_z, far_z, far_back = slab(1), slab(-1), slab(2), slab(-2)
    x_low = lax.rem(me + peers - 1, peers)
    x_high = lax.rem(me + 1, peers)
    square = peers == 4
    if square:
        hi, lo = lax.div(me, 2), lax.rem(me, 2)
        peer = [me, me + 1 - 2 * lo, me + 2 - 4 * hi, 3 - me]
    else:
        peer = [lax.rem(me + k, peers) for k in range(peers)]

    barrier = pltpu.get_barrier_semaphore()
    greeted = [sib, near_z, far_z, far_back]
    for z in greeted:
        pl.semaphore_signal(barrier, inc=1, device_id=(me, z), device_id_type=MESH)
    for k in range(1, peers):
        pl.semaphore_signal(
            barrier, inc=1, device_id=(peer[k], sl), device_id_type=MESH
        )

    def pull(k):
        start = pl.multiple_of(peer[k] * wide, 8)
        return pltpu.make_async_copy(
            states.at[:, :, pl.ds(start, wide), :], stage.at[k], in_sem.at[k]
        )

    for k in [*range(1, peers), 0]:
        pull(k).start()
    core_copy = pltpu.make_async_copy(
        core.at[:, pl.ds(pl.multiple_of(me * wide, 8), wide), :], core_v, core_sem
    )
    core_copy.start()

    weights = [occ[s].astype(jnp.float32) * (1.0 / denominator) for s in range(nst)]

    def term(k, p, at):
        total = None
        for s in range(nst):
            value = stage[k, s, p, pl.ds(at, rows), :]
            part = (weights[s] * value) * value
            total = part if total is None else total + part
        return total

    def remote(source, target, sems, device):
        return pltpu.make_async_remote_copy(
            src_ref=source,
            dst_ref=target,
            send_sem=sems[0],
            recv_sem=sems[1],
            device_id=device,
            device_id_type=MESH,
        )

    def share(c, k):
        sems = rs_send.at[k - 1, c], rs_recv.at[k - 1, c]
        return remote(snd.at[c, k - 1], rcv.at[c, k - 1], sems, (peer[k], sl))

    def planes(c, k):
        span = pl.ds(edge + c * rows, rows)
        step = (1, -1, 2)[k]
        source = dens.at[pl.ds(2 * nz, nz), span, :]
        target = dens.at[pl.ds((2 - step * way) * nz, nz), span, :]
        return remote(source, target, (z_send.at[k, c], z_recv.at[k, c]), (me, (sib, near_z, far_z)[k]))

    def fluxes(c):
        span = pl.ds(c * rows, rows)
        source = fz.at[pl.ds(nz, nz), span, :]
        target = fz.at[pl.ds((1 - way) * nz, nz), span, :]
        return remote(source, target, (f_send.at[c], f_recv.at[c]), (me, sib))

    def corners():
        return remote(rim_in.at[0], rim_near, (c_send, c_recv), (me, near_z))

    def sides(field, side):
        sems = x_send.at[field, side], x_recv.at[field, side]
        return remote(
            rim_out.at[field, side], rim_in.at[field, side], sems, ((x_low, x_high)[side], sl)
        )

    started, waited = [], set()

    def start(copy):
        copy.start()
        started.append(copy)

    def arrived(name, make, *where):
        if (name, where) not in waited:
            waited.add((name, where))
            make(*where).wait_recv()

    def landed(c, k):
        arrived("planes", planes, c, k)

    sent = set()

    def far(c):
        send(c, (peers - 1,))

    def send(c, targets=None):
        targets = [k for k in targets or range(peers - 1, 0, -1) if (c, k) not in sent]
        if not sent:
            for k in range(peers - 1, 0, -1):
                pull(k).wait()
        for k in targets:
            for p in range(nz):
                snd[c, k - 1, p] = term(k, p, c * rows)
        if not sent:
            pl.semaphore_wait(barrier, peers - 1 + len(greeted))
        for k in targets:
            start(share(c, k))
            sent.add((c, k))

    def gather(c):
        at = c * rows
        if c == order[0]:
            pull(0).wait()
            core_copy.wait()
        for k in range(1, peers):
            share(c, k).wait_recv()
        for p in range(nz):
            total = term(0, p, at) + core_v[p, pl.ds(at, rows), :]
            for k in range(1, peers):
                total = total + rcv[c, k - 1, p]
            dens[2 * nz + p, pl.ds(edge + at, rows), :] = total
            if c == 0:
                rim_out[0, 0, p] = total[:2]
            if c == chunks - 1:
                rim_out[0, 1, p] = total[rows - 2 :]
        if c == 0:
            start(sides(0, 0))
        if c == chunks - 1:
            start(sides(0, 1))
        for k in (2, 1, 0):
            start(planes(c, k))

    def edges(field):
        ref, base = ((dens, 2 * nz), (fx, 0))[field]
        for side in (0, 1):
            arrived("sides", sides, field, side)
        if field == 0:
            start(corners())
        for p in range(nz):
            ref[base + p, pl.ds(edge + wide, 2), :] = rim_in[field, 0, p]
            ref[base + p, pl.ds(edge - 2, 2), :] = rim_in[field, 1, p]

    def outer(_):
        corners().wait_recv()
        base = (2 - way) * nz
        for p in range(nz):
            dens[base + p, pl.ds(edge + wide, 2), :] = rim_near[0, p]
            dens[base + p, pl.ds(edge - 2, 2), :] = rim_near[1, p]

    def fields(plane, at):
        inner = pl.ds(at + edge, rows)
        n = dens[plane, inner, :]
        low2, low1 = dens[plane - 2, inner, :], dens[plane - 1, inner, :]
        high1, high2 = dens[plane + 1, inner, :], dens[plane + 2, inner, :]
        grad_z = five_point(low2, low1, high1, high2)
        grad_x = deriv_x(dens[pl.ds(plane, 1), pl.ds(at, rows + 2 * edge), :])[0]
        grad_y = deriv_y(n)
        g = grad_z * grad_z + grad_x * grad_x + grad_y * grad_y
        e_rho, e_grad = pbe_derivs(n, g)
        return e_rho, 2.0 * e_grad, grad_z, grad_x, grad_y

    def energy(c):
        landed(c, 0)
        landed(c, 1)
        at = c * rows
        for p in range(nz):
            e_rho, twice, grad_z, grad_x, grad_y = fields(2 * nz + p, at)
            fz[nz + p, pl.ds(at, rows), :] = twice * grad_z
            flux_x = twice * grad_x
            fx[p, pl.ds(at + edge, rows), :] = flux_x
            if c == 0:
                rim_out[1, 0, p] = flux_x[:2]
            if c == chunks - 1:
                rim_out[1, 1, p] = flux_x[rows - 2 :]
            out[p, pl.ds(at, rows), :] = e_rho - deriv_y(twice * grad_y)
        start(fluxes(c))
        if c == 0:
            start(sides(1, 0))
        if c == chunks - 1:
            start(sides(1, 1))

    def beyond(c):
        landed(c, 2)
        for d in range(max(c - 1, 0), min(c + 2, chunks)):
            landed(d, 1)
        at = c * rows
        for p in range(nz):
            _, twice, grad_z, _, _ = fields((2 - way) * nz + p, at)
            fz[(1 - way) * nz + p, pl.ds(at, rows), :] = twice * grad_z

    def diverge(c):
        fluxes(c).wait_recv()
        at = c * rows
        span = pl.ds(at, rows)
        for p in range(nz):
            div_z = five_point(
                fz[nz + p - 2, span, :], fz[nz + p - 1, span, :], fz[nz + p + 1, span, :], fz[nz + p + 2, span, :]
            )
            div_x = deriv_x(fx[p : p + 1, pl.ds(at, rows + 2 * edge), :])[0]
            out[p, span, :] = out[p, span, :] - (div_z + div_x)

    order = [c for name, c in steps if name == "send"]
    act = dict(far=far, send=send, gather=gather, edges=edges, outer=outer, energy=energy, beyond=beyond, diverge=diverge)
    for name, c in steps:
        act[name](c)
    for copy in started:
        copy.wait_send()


def shards(peers, slabs, states, occupations, core_density):
    nst, nz, full, deep = states.shape
    wide = full // peers
    rows = edge
    chunks = wide // rows
    steps = plan(chunks)
    f32 = jnp.float32
    dma = pltpu.SemaphoreType.DMA
    return pl.pallas_call(
        functools.partial(kernel, peers, slabs, rows, steps),
        out_shape=pltpu.VMEM((nz, wide, deep), f32),
        in_specs=[
            pl.BlockSpec(memory_space=pl.ANY),
            pl.BlockSpec(memory_space=pltpu.SMEM),
            pl.BlockSpec(memory_space=pl.ANY),
        ],
        out_specs=pl.BlockSpec(memory_space=pltpu.VMEM),
        scratch_shapes=[
            pltpu.VMEM((peers, nst, nz, wide, deep), f32),
            pltpu.VMEM((nz, wide, deep), f32),
            pltpu.VMEM((chunks, peers - 1, nz, rows, deep), f32),
            pltpu.VMEM((chunks, peers - 1, nz, rows, deep), f32),
            pltpu.VMEM((5 * nz, wide + 2 * edge, deep), f32),
            pltpu.VMEM((3 * nz, wide, deep), f32),
            pltpu.VMEM((nz, wide + 2 * edge, deep), f32),
            pltpu.VMEM((2, 2, nz, 2, deep), f32),
            pltpu.VMEM((2, 2, nz, 2, deep), f32),
            pltpu.VMEM((2, nz, 2, deep), f32),
            dma((peers,)),
            dma,
            dma((peers - 1, chunks)),
            dma((peers - 1, chunks)),
            dma((3, chunks)),
            dma((3, chunks)),
            dma((chunks,)),
            dma((chunks,)),
            dma((2, 2)),
            dma((2, 2)),
            dma,
            dma,
        ],
        compiler_params=pltpu.CompilerParams(
            collective_id=0, has_side_effects=True, vmem_limit_bytes=67043328 - 1024 * 1024
        ),
    )(states, occupations, core_density)


def solution(mesh):
    return jax.shard_map(
        functools.partial(shards, mesh.shape["interval"], mesh.shape["slab"]),
        mesh=mesh,
        in_specs=(P("interval", "slab", None, None), P("interval"), P("slab", None, None)),
        out_specs=P("slab", "interval", None),
        check_vma=False,
    )
```

```python
import functools
import math

import jax
import jax.numpy as jnp
from jax import lax
from jax.experimental import pallas as pl
from jax.experimental.pallas import tpu as pltpu
from jax.sharding import PartitionSpec as P

spacing = 0.25
denominator = 64.0
pbe_kappa = 0.804
pbe_mu = 0.2195149727645171
pbe_beta = 0.06672455060314922
pw_alpha = 0.0310907
pbe_gamma = (1.0 - math.log(2.0)) / math.pi**2
MESH = pl.DeviceIdType.MESH
edge = 8


def five_point(low2, low1, high1, high2):
    return (8.0 * (high1 - low1) - (high2 - low2)) * (1.0 / (12.0 * spacing))


def deriv_y(field):
    axis = field.ndim - 1
    count = field.shape[axis]
    return five_point(
        pltpu.roll(field, 2, axis),
        pltpu.roll(field, 1, axis),
        pltpu.roll(field, count - 1, axis),
        pltpu.roll(field, count - 2, axis),
    )


def deriv_x(tall):
    return five_point(
        tall[:, edge - 2 : -edge - 2],
        tall[:, edge - 1 : -edge - 1],
        tall[:, edge + 1 : 1 - edge],
        tall[:, edge + 2 : 2 - edge],
    )


def pbe_derivs(n, g):
    k_one = (3.0 * math.pi**2) ** (1.0 / 3.0)
    ex_one = -0.75 * (3.0 / math.pi) ** (1.0 / 3.0)
    r_one = (3.0 / (4.0 * math.pi)) ** (1.0 / 3.0)
    s_one = 1.0 / (4.0 * k_one**2)
    t_one = math.pi / (16.0 * k_one)
    ratio = pbe_beta / pbe_gamma
    inv_six = jnp.exp(jnp.log(n) * (-1.0 / 6.0))
    inv = inv_six * inv_six
    inv2 = inv * inv
    inv4 = inv2 * inv2
    cube = n * inv2
    s_sq = (s_one * g) * (inv4 * inv4)
    u_inv = 1.0 / (1.0 + (pbe_mu / pbe_kappa) * s_sq)
    f_exch = (1.0 + pbe_kappa) - pbe_kappa * u_inv
    f_slope = pbe_mu * u_inv * u_inv
    ex_rho = (ex_one * cube) * ((4.0 / 3.0) * f_exch - (8.0 / 3.0) * f_slope * s_sq)

    radius = r_one * inv
    root = math.sqrt(r_one) * inv_six
    two_a = 2.0 * pw_alpha
    lower = (two_a * root) * (
        7.5957 + root * (3.5876 + root * (1.6382 + root * 0.49294))
    )
    slope = (two_a * root) * (
        0.5 * 7.5957 + root * (3.5876 + root * (1.5 * 1.6382 + root * (2.0 * 0.49294)))
    )
    pair_inv = 1.0 / (lower * (lower + 1.0))
    log_term = jnp.log(1.0 + (lower + 1.0) * pair_inv)
    front = two_a + (two_a * 0.2137) * radius
    e_corr = -front * log_term
    n_ec = (1.0 / 3.0) * ((two_a * 0.2137) * radius * log_term - front * slope * pair_inv)

    grown = jnp.exp(e_corr * (-1.0 / pbe_gamma))
    factor = ratio / (grown - 1.0)
    t_sq = (t_one * g) * (inv4 * inv2 * inv)
    y = factor * t_sq
    lift = 1.0 + y
    den = lift + y * y
    add = (ratio * t_sq) * lift
    full = den + add
    inv_full = 1.0 / (den * full)
    h_term = pbe_gamma * jnp.log(1.0 + add * (full * inv_full))
    h_t = (pbe_beta * inv_full) * (1.0 + 2.0 * y)
    h_ec = -(y * y) * (y * (2.0 + y)) * inv_full * grown
    e_rho = ex_rho + e_corr + h_term + n_ec + h_ec * n_ec - (7.0 / 3.0) * (t_sq * h_t)
    e_grad = inv4 * (t_one * h_t + (ex_one * s_one) * f_slope)
    return e_rho, e_grad


def plan(chunks, ahead=4, turn=5):
    order = []
    for i in range((chunks + 1) // 2):
        order += [i] if i == chunks - 1 - i else [i, chunks - 1 - i]
    last = order[-1]
    calm = [c for c in order if abs(c - last) > 1]
    late = [c for c in order if abs(c - last) == 1]
    turn = min(turn, chunks)
    steps = [("send", c) for c in order[:ahead]]
    for i, c in enumerate(order):
        steps.append(("gather", c))
        steps += [("send", d) for d in order[ahead + i : ahead + i + 1]]
        steps += [("edges", 0)] if i == turn - 1 else []
    steps += [("energy", c) for c in calm + late]
    steps += [("beyond", c) for c in calm if 0 < c < chunks - 1]
    steps += [("outer", 0)] + [("beyond", c) for c in calm if c in (0, chunks - 1)]
    done = [c for c in calm if 0 < c < chunks - 1]
    steps += [("diverge", c) for c in done]
    steps += [("energy", last), ("edges", 1)] + [("diverge", c) for c in calm if c not in done]
    for c in late + [last]:
        steps += [("beyond", c), ("diverge", c)]
    return steps


def kernel(
    peers, slabs, rows, steps,
    states, occ, core, out,
    stage, core_v, snd, rcv, dens, fz, fx, rim_out, rim_in, rim_near,
    in_sem, core_sem, rs_send, rs_recv,
    z_send, z_recv, f_send, f_recv, x_send, x_recv, c_send, c_recv,
):
    nst, nz, wide = stage.shape[1], stage.shape[2], stage.shape[3]
    chunks = wide // rows
    me = lax.axis_index("interval")
    sl = lax.axis_index("slab")
    odd = lax.rem(sl, 2)
    way = 1 - 2 * odd

    def slab(step):
        return lax.rem(sl + step * way + slabs, slabs)

    sib, near_z, far_z, far_back = slab(1), slab(-1), slab(2), slab(-2)
    x_low = lax.rem(me + peers - 1, peers)
    x_high = lax.rem(me + 1, peers)
    square = peers == 4
    if square:
        hi, lo = lax.div(me, 2), lax.rem(me, 2)
        peer = [me, me + 1 - 2 * lo, me + 2 - 4 * hi, 3 - me]
    else:
        peer = [lax.rem(me + k, peers) for k in range(peers)]

    barrier = pltpu.get_barrier_semaphore()
    greeted = [sib, near_z, far_z, far_back]
    for z in greeted:
        pl.semaphore_signal(barrier, inc=1, device_id=(me, z), device_id_type=MESH)
    for k in range(1, peers):
        pl.semaphore_signal(
            barrier, inc=1, device_id=(peer[k], sl), device_id_type=MESH
        )

    def pull(k):
        start = pl.multiple_of(peer[k] * wide, 8)
        return pltpu.make_async_copy(
            states.at[:, :, pl.ds(start, wide), :], stage.at[k], in_sem.at[k]
        )

    for k in [*range(1, peers), 0]:
        pull(k).start()
    core_copy = pltpu.make_async_copy(
        core.at[:, pl.ds(pl.multiple_of(me * wide, 8), wide), :], core_v, core_sem
    )
    core_copy.start()

    weights = [occ[s].astype(jnp.float32) * (1.0 / denominator) for s in range(nst)]

    def term(k, p, at):
        total = None
        for s in range(nst):
            value = stage[k, s, p, pl.ds(at, rows), :]
            part = (weights[s] * value) * value
            total = part if total is None else total + part
        return total

    def remote(source, target, sems, device):
        return pltpu.make_async_remote_copy(
            src_ref=source,
            dst_ref=target,
            send_sem=sems[0],
            recv_sem=sems[1],
            device_id=device,
            device_id_type=MESH,
        )

    def share(c, k):
        sems = rs_send.at[k - 1, c], rs_recv.at[k - 1, c]
        return remote(snd.at[c, k - 1], rcv.at[c, k - 1], sems, (peer[k], sl))

    def planes(c, k):
        span = pl.ds(edge + c * rows, rows)
        step = (1, -1, 2)[k]
        source = dens.at[pl.ds(2 * nz, nz), span, :]
        target = dens.at[pl.ds((2 - step * way) * nz, nz), span, :]
        return remote(source, target, (z_send.at[k, c], z_recv.at[k, c]), (me, (sib, near_z, far_z)[k]))

    def fluxes(c):
        span = pl.ds(c * rows, rows)
        source = fz.at[pl.ds(nz, nz), span, :]
        target = fz.at[pl.ds((1 - way) * nz, nz), span, :]
        return remote(source, target, (f_send.at[c], f_recv.at[c]), (me, sib))

    def corners():
        return remote(rim_in.at[0], rim_near, (c_send, c_recv), (me, near_z))

    def sides(field, side):
        sems = x_send.at[field, side], x_recv.at[field, side]
        return remote(
            rim_out.at[field, side], rim_in.at[field, side], sems, ((x_low, x_high)[side], sl)
        )

    started, waited = [], set()

    def start(copy):
        copy.start()
        started.append(copy)

    def arrived(name, make, *where):
        if (name, where) not in waited:
            waited.add((name, where))
            make(*where).wait_recv()

    def landed(c, k):
        arrived("planes", planes, c, k)

    def send(c):
        if c == order[0]:
            for k in range(peers - 1, 0, -1):
                pull(k).wait()
        for k in range(peers - 1, 0, -1):
            for p in range(nz):
                snd[c, k - 1, p] = term(k, p, c * rows)
            if c == order[0] and k == peers - 1:
                pl.semaphore_wait(barrier, peers - 1 + len(greeted))
            start(share(c, k))

    def gather(c):
        at = c * rows
        if c == order[0]:
            pull(0).wait()
            core_copy.wait()
        for k in range(1, peers):
            share(c, k).wait_recv()
        for p in range(nz):
            total = term(0, p, at) + core_v[p, pl.ds(at, rows), :]
            for k in range(1, peers):
                total = total + rcv[c, k - 1, p]
            dens[2 * nz + p, pl.ds(edge + at, rows), :] = total
            if c == 0:
                rim_out[0, 0, p] = total[:2]
            if c == chunks - 1:
                rim_out[0, 1, p] = total[rows - 2 :]
        if c == 0:
            start(sides(0, 0))
        if c == chunks - 1:
            start(sides(0, 1))
        for k in (2, 1, 0):
            start(planes(c, k))

    def edges(field):
        ref, base = ((dens, 2 * nz), (fx, 0))[field]
        for side in (0, 1):
            arrived("sides", sides, field, side)
        if field == 0:
            start(corners())
        for p in range(nz):
            ref[base + p, pl.ds(edge + wide, 2), :] = rim_in[field, 0, p]
            ref[base + p, pl.ds(edge - 2, 2), :] = rim_in[field, 1, p]

    def outer(_):
        corners().wait_recv()
        base = (2 - way) * nz
        for p in range(nz):
            dens[base + p, pl.ds(edge + wide, 2), :] = rim_near[0, p]
            dens[base + p, pl.ds(edge - 2, 2), :] = rim_near[1, p]

    def fields(plane, at):
        inner = pl.ds(at + edge, rows)
        n = dens[plane, inner, :]
        low2, low1 = dens[plane - 2, inner, :], dens[plane - 1, inner, :]
        high1, high2 = dens[plane + 1, inner, :], dens[plane + 2, inner, :]
        grad_z = five_point(low2, low1, high1, high2)
        grad_x = deriv_x(dens[pl.ds(plane, 1), pl.ds(at, rows + 2 * edge), :])[0]
        grad_y = deriv_y(n)
        g = grad_z * grad_z + grad_x * grad_x + grad_y * grad_y
        e_rho, e_grad = pbe_derivs(n, g)
        return e_rho, 2.0 * e_grad, grad_z, grad_x, grad_y

    def energy(c):
        landed(c, 0)
        landed(c, 1)
        at = c * rows
        for p in range(nz):
            e_rho, twice, grad_z, grad_x, grad_y = fields(2 * nz + p, at)
            fz[nz + p, pl.ds(at, rows), :] = twice * grad_z
            flux_x = twice * grad_x
            fx[p, pl.ds(at + edge, rows), :] = flux_x
            if c == 0:
                rim_out[1, 0, p] = flux_x[:2]
            if c == chunks - 1:
                rim_out[1, 1, p] = flux_x[rows - 2 :]
            out[p, pl.ds(at, rows), :] = e_rho - deriv_y(twice * grad_y)
        start(fluxes(c))
        if c == 0:
            start(sides(1, 0))
        if c == chunks - 1:
            start(sides(1, 1))

    def beyond(c):
        landed(c, 2)
        for d in range(max(c - 1, 0), min(c + 2, chunks)):
            landed(d, 1)
        at = c * rows
        for p in range(nz):
            _, twice, grad_z, _, _ = fields((2 - way) * nz + p, at)
            fz[(1 - way) * nz + p, pl.ds(at, rows), :] = twice * grad_z

    def diverge(c):
        fluxes(c).wait_recv()
        at = c * rows
        span = pl.ds(at, rows)
        for p in range(nz):
            div_z = five_point(
                fz[nz + p - 2, span, :], fz[nz + p - 1, span, :], fz[nz + p + 1, span, :], fz[nz + p + 2, span, :]
            )
            div_x = deriv_x(fx[p : p + 1, pl.ds(at, rows + 2 * edge), :])[0]
            out[p, span, :] = out[p, span, :] - (div_z + div_x)

    order = [c for name, c in steps if name == "send"]
    act = dict(send=send, gather=gather, edges=edges, outer=outer, energy=energy, beyond=beyond, diverge=diverge)
    for name, c in steps:
        act[name](c)
    for copy in started:
        copy.wait_send()


def shards(peers, slabs, states, occupations, core_density):
    nst, nz, full, deep = states.shape
    wide = full // peers
    rows = edge
    chunks = wide // rows
    steps = plan(chunks)
    f32 = jnp.float32
    dma = pltpu.SemaphoreType.DMA
    return pl.pallas_call(
        functools.partial(kernel, peers, slabs, rows, steps),
        out_shape=pltpu.VMEM((nz, wide, deep), f32),
        in_specs=[
            pl.BlockSpec(memory_space=pl.ANY),
            pl.BlockSpec(memory_space=pltpu.SMEM),
            pl.BlockSpec(memory_space=pl.ANY),
        ],
        out_specs=pl.BlockSpec(memory_space=pltpu.VMEM),
        scratch_shapes=[
            pltpu.VMEM((peers, nst, nz, wide, deep), f32),
            pltpu.VMEM((nz, wide, deep), f32),
            pltpu.VMEM((chunks, peers - 1, nz, rows, deep), f32),
            pltpu.VMEM((chunks, peers - 1, nz, rows, deep), f32),
            pltpu.VMEM((5 * nz, wide + 2 * edge, deep), f32),
            pltpu.VMEM((3 * nz, wide, deep), f32),
            pltpu.VMEM((nz, wide + 2 * edge, deep), f32),
            pltpu.VMEM((2, 2, nz, 2, deep), f32),
            pltpu.VMEM((2, 2, nz, 2, deep), f32),
            pltpu.VMEM((2, nz, 2, deep), f32),
            dma((peers,)),
            dma,
            dma((peers - 1, chunks)),
            dma((peers - 1, chunks)),
            dma((3, chunks)),
            dma((3, chunks)),
            dma((chunks,)),
            dma((chunks,)),
            dma((2, 2)),
            dma((2, 2)),
            dma,
            dma,
        ],
        compiler_params=pltpu.CompilerParams(
            collective_id=0, has_side_effects=True, vmem_limit_bytes=67043328 - 1024 * 1024
        ),
    )(states, occupations, core_density)


def solution(mesh):
    return jax.shard_map(
        functools.partial(shards, mesh.shape["interval"], mesh.shape["slab"]),
        mesh=mesh,
        in_specs=(P("interval", "slab", None, None), P("interval"), P("slab", None, None)),
        out_specs=P("slab", "interval", None),
        check_vma=False,
    )
```

```python
import functools
import math

import jax
import jax.numpy as jnp
from jax import lax
from jax.experimental import pallas as pl
from jax.experimental.pallas import tpu as pltpu
from jax.sharding import PartitionSpec as P

spacing = 0.25
denominator = 64.0
pbe_kappa = 0.804
pbe_mu = 0.2195149727645171
pbe_beta = 0.06672455060314922
pw_alpha = 0.0310907
pbe_gamma = (1.0 - math.log(2.0)) / math.pi**2
MESH = pl.DeviceIdType.MESH
edge = 8


def five_point(low2, low1, high1, high2):
    return (8.0 * (high1 - low1) - (high2 - low2)) * (1.0 / (12.0 * spacing))


def deriv_y(field):
    axis = field.ndim - 1
    count = field.shape[axis]
    return five_point(
        pltpu.roll(field, 2, axis),
        pltpu.roll(field, 1, axis),
        pltpu.roll(field, count - 1, axis),
        pltpu.roll(field, count - 2, axis),
    )


def deriv_x(tall):
    return five_point(
        tall[:, edge - 2 : -edge - 2],
        tall[:, edge - 1 : -edge - 1],
        tall[:, edge + 1 : 1 - edge],
        tall[:, edge + 2 : 2 - edge],
    )


def pbe_derivs(n, g):
    k_one = (3.0 * math.pi**2) ** (1.0 / 3.0)
    ex_one = -0.75 * (3.0 / math.pi) ** (1.0 / 3.0)
    r_one = (3.0 / (4.0 * math.pi)) ** (1.0 / 3.0)
    s_one = 1.0 / (4.0 * k_one**2)
    t_one = math.pi / (16.0 * k_one)
    ratio = pbe_beta / pbe_gamma
    inv_six = jnp.exp(jnp.log(n) * (-1.0 / 6.0))
    inv = inv_six * inv_six
    inv2 = inv * inv
    inv4 = inv2 * inv2
    cube = n * inv2
    s_sq = (s_one * g) * (inv4 * inv4)
    u_inv = 1.0 / (1.0 + (pbe_mu / pbe_kappa) * s_sq)
    f_exch = (1.0 + pbe_kappa) - pbe_kappa * u_inv
    f_slope = pbe_mu * u_inv * u_inv
    ex_rho = (ex_one * cube) * ((4.0 / 3.0) * f_exch - (8.0 / 3.0) * f_slope * s_sq)

    radius = r_one * inv
    root = math.sqrt(r_one) * inv_six
    two_a = 2.0 * pw_alpha
    lower = (two_a * root) * (
        7.5957 + root * (3.5876 + root * (1.6382 + root * 0.49294))
    )
    slope = (two_a * root) * (
        0.5 * 7.5957 + root * (3.5876 + root * (1.5 * 1.6382 + root * (2.0 * 0.49294)))
    )
    pair_inv = 1.0 / (lower * (lower + 1.0))
    log_term = jnp.log(1.0 + (lower + 1.0) * pair_inv)
    front = two_a + (two_a * 0.2137) * radius
    e_corr = -front * log_term
    n_ec = (1.0 / 3.0) * ((two_a * 0.2137) * radius * log_term - front * slope * pair_inv)

    grown = jnp.exp(e_corr * (-1.0 / pbe_gamma))
    factor = ratio / (grown - 1.0)
    t_sq = (t_one * g) * (inv4 * inv2 * inv)
    y = factor * t_sq
    lift = 1.0 + y
    den = lift + y * y
    add = (ratio * t_sq) * lift
    full = den + add
    inv_full = 1.0 / (den * full)
    h_term = pbe_gamma * jnp.log(1.0 + add * (full * inv_full))
    h_t = (pbe_beta * inv_full) * (1.0 + 2.0 * y)
    h_ec = -(y * y) * (y * (2.0 + y)) * inv_full * grown
    e_rho = ex_rho + e_corr + h_term + n_ec + h_ec * n_ec - (7.0 / 3.0) * (t_sq * h_t)
    e_grad = inv4 * (t_one * h_t + (ex_one * s_one) * f_slope)
    return e_rho, e_grad


def plan(chunks, ahead=4, turn=5):
    order = []
    for i in range((chunks + 1) // 2):
        order += [i] if i == chunks - 1 - i else [i, chunks - 1 - i]
    last = order[-1]
    calm = [c for c in order if abs(c - last) > 1]
    late = [c for c in order if abs(c - last) == 1]
    turn = min(turn, chunks)
    steps = [("send", c) for c in order[:ahead]]
    for i, c in enumerate(order):
        steps.append(("gather", c))
        steps += [("send", d) for d in order[ahead + i : ahead + i + 1]]
        steps += [("edges", 0)] if i == turn - 1 else []
    steps += [("energy", c) for c in calm + late]
    steps += [("beyond", c) for c in calm if 0 < c < chunks - 1]
    steps += [("outer", 0)] + [("beyond", c) for c in calm if c in (0, chunks - 1)]
    done = [c for c in calm if 0 < c < chunks - 1]
    steps += [("diverge", c) for c in done]
    steps += [("energy", last), ("edges", 1)] + [("diverge", c) for c in calm if c not in done]
    for c in late + [last]:
        steps += [("beyond", c), ("diverge", c)]
    return steps


def kernel(
    peers, slabs, rows, steps,
    states, occ, core, out,
    stage, core_v, snd, rcv, dens, fz, fx, rim_out, rim_in, rim_near,
    in_sem, core_sem, rs_send, rs_recv,
    z_send, z_recv, f_send, f_recv, x_send, x_recv, c_send, c_recv,
):
    nst, nz, wide = stage.shape[1], stage.shape[2], stage.shape[3]
    chunks = wide // rows
    me = lax.axis_index("interval")
    sl = lax.axis_index("slab")
    odd = lax.rem(sl, 2)
    way = 1 - 2 * odd

    def slab(step):
        return lax.rem(sl + step * way + slabs, slabs)

    sib, near_z, far_z, far_back = slab(1), slab(-1), slab(2), slab(-2)
    x_low = lax.rem(me + peers - 1, peers)
    x_high = lax.rem(me + 1, peers)
    square = peers == 4
    if square:
        hi, lo = lax.div(me, 2), lax.rem(me, 2)
        peer = [me, me + 1 - 2 * lo, me + 2 - 4 * hi, 3 - me]
    else:
        peer = [lax.rem(me + k, peers) for k in range(peers)]

    barrier = pltpu.get_barrier_semaphore()
    greeted = [sib, near_z, far_z, far_back]
    for z in greeted:
        pl.semaphore_signal(barrier, inc=1, device_id=(me, z), device_id_type=MESH)
    for k in range(1, peers):
        pl.semaphore_signal(
            barrier, inc=1, device_id=(peer[k], sl), device_id_type=MESH
        )

    def pull(k):
        start = pl.multiple_of(peer[k] * wide, 8)
        return pltpu.make_async_copy(
            states.at[:, :, pl.ds(start, wide), :], stage.at[k], in_sem.at[k]
        )

    for k in [*range(1, peers), 0]:
        pull(k).start()
    core_copy = pltpu.make_async_copy(
        core.at[:, pl.ds(pl.multiple_of(me * wide, 8), wide), :], core_v, core_sem
    )
    core_copy.start()

    weights = [occ[s].astype(jnp.float32) * (1.0 / denominator) for s in range(nst)]

    def term(k, p, at):
        total = None
        for s in range(nst):
            value = stage[k, s, p, pl.ds(at, rows), :]
            part = (weights[s] * value) * value
            total = part if total is None else total + part
        return total

    def remote(source, target, sems, device):
        return pltpu.make_async_remote_copy(
            src_ref=source,
            dst_ref=target,
            send_sem=sems[0],
            recv_sem=sems[1],
            device_id=device,
            device_id_type=MESH,
        )

    def share(c, k):
        sems = rs_send.at[k - 1, c], rs_recv.at[k - 1, c]
        return remote(snd.at[c, k - 1], rcv.at[c, k - 1], sems, (peer[k], sl))

    def planes(c, k):
        span = pl.ds(edge + c * rows, rows)
        step = (1, -1, 2)[k]
        source = dens.at[pl.ds(2 * nz, nz), span, :]
        target = dens.at[pl.ds((2 - step * way) * nz, nz), span, :]
        return remote(source, target, (z_send.at[k, c], z_recv.at[k, c]), (me, (sib, near_z, far_z)[k]))

    def fluxes(c):
        span = pl.ds(c * rows, rows)
        source = fz.at[pl.ds(nz, nz), span, :]
        target = fz.at[pl.ds((1 - way) * nz, nz), span, :]
        return remote(source, target, (f_send.at[c], f_recv.at[c]), (me, sib))

    def corners():
        return remote(rim_in.at[0], rim_near, (c_send, c_recv), (me, near_z))

    def sides(field, side):
        sems = x_send.at[field, side], x_recv.at[field, side]
        return remote(
            rim_out.at[field, side], rim_in.at[field, side], sems, ((x_low, x_high)[side], sl)
        )

    started, waited = [], set()

    def start(copy):
        copy.start()
        started.append(copy)

    def arrived(name, make, *where):
        if (name, where) not in waited:
            waited.add((name, where))
            make(*where).wait_recv()

    def landed(c, k):
        arrived("planes", planes, c, k)

    def send(c):
        if c == order[0]:
            for k in range(peers - 1, 0, -1):
                pull(k).wait()
        for k in range(peers - 1, 0, -1):
            for p in range(nz):
                snd[c, k - 1, p] = term(k, p, c * rows)
            if c == order[0] and k == peers - 1:
                pl.semaphore_wait(barrier, peers - 1 + len(greeted))
            start(share(c, k))

    def gather(c):
        at = c * rows
        if c == order[0]:
            pull(0).wait()
            core_copy.wait()
        for k in range(1, peers):
            share(c, k).wait_recv()
        for p in range(nz):
            total = term(0, p, at) + core_v[p, pl.ds(at, rows), :]
            for k in range(1, peers):
                total = total + rcv[c, k - 1, p]
            dens[2 * nz + p, pl.ds(edge + at, rows), :] = total
            if c == 0:
                rim_out[0, 0, p] = total[:2]
            if c == chunks - 1:
                rim_out[0, 1, p] = total[rows - 2 :]
        if c == 0:
            start(sides(0, 0))
        if c == chunks - 1:
            start(sides(0, 1))
        for k in (0, 2, 1) if c == order[-1] else (2, 1, 0):
            start(planes(c, k))

    def edges(field):
        ref, base = ((dens, 2 * nz), (fx, 0))[field]
        for side in (0, 1):
            arrived("sides", sides, field, side)
        if field == 0:
            start(corners())
        for p in range(nz):
            ref[base + p, pl.ds(edge + wide, 2), :] = rim_in[field, 0, p]
            ref[base + p, pl.ds(edge - 2, 2), :] = rim_in[field, 1, p]

    def outer(_):
        corners().wait_recv()
        base = (2 - way) * nz
        for p in range(nz):
            dens[base + p, pl.ds(edge + wide, 2), :] = rim_near[0, p]
            dens[base + p, pl.ds(edge - 2, 2), :] = rim_near[1, p]

    def fields(plane, at):
        inner = pl.ds(at + edge, rows)
        n = dens[plane, inner, :]
        low2, low1 = dens[plane - 2, inner, :], dens[plane - 1, inner, :]
        high1, high2 = dens[plane + 1, inner, :], dens[plane + 2, inner, :]
        grad_z = five_point(low2, low1, high1, high2)
        grad_x = deriv_x(dens[pl.ds(plane, 1), pl.ds(at, rows + 2 * edge), :])[0]
        grad_y = deriv_y(n)
        g = grad_z * grad_z + grad_x * grad_x + grad_y * grad_y
        e_rho, e_grad = pbe_derivs(n, g)
        return e_rho, 2.0 * e_grad, grad_z, grad_x, grad_y

    def energy(c):
        landed(c, 0)
        landed(c, 1)
        at = c * rows
        for p in range(nz):
            e_rho, twice, grad_z, grad_x, grad_y = fields(2 * nz + p, at)
            fz[nz + p, pl.ds(at, rows), :] = twice * grad_z
            flux_x = twice * grad_x
            fx[p, pl.ds(at + edge, rows), :] = flux_x
            if c == 0:
                rim_out[1, 0, p] = flux_x[:2]
            if c == chunks - 1:
                rim_out[1, 1, p] = flux_x[rows - 2 :]
            out[p, pl.ds(at, rows), :] = e_rho - deriv_y(twice * grad_y)
        start(fluxes(c))
        if c == 0:
            start(sides(1, 0))
        if c == chunks - 1:
            start(sides(1, 1))

    def beyond(c):
        landed(c, 2)
        for d in range(max(c - 1, 0), min(c + 2, chunks)):
            landed(d, 1)
        at = c * rows
        for p in range(nz):
            _, twice, grad_z, _, _ = fields((2 - way) * nz + p, at)
            fz[(1 - way) * nz + p, pl.ds(at, rows), :] = twice * grad_z

    def diverge(c):
        fluxes(c).wait_recv()
        at = c * rows
        span = pl.ds(at, rows)
        for p in range(nz):
            div_z = five_point(
                fz[nz + p - 2, span, :], fz[nz + p - 1, span, :], fz[nz + p + 1, span, :], fz[nz + p + 2, span, :]
            )
            div_x = deriv_x(fx[p : p + 1, pl.ds(at, rows + 2 * edge), :])[0]
            out[p, span, :] = out[p, span, :] - (div_z + div_x)

    order = [c for name, c in steps if name == "send"]
    act = dict(send=send, gather=gather, edges=edges, outer=outer, energy=energy, beyond=beyond, diverge=diverge)
    for name, c in steps:
        act[name](c)
    for copy in started:
        copy.wait_send()


def shards(peers, slabs, states, occupations, core_density):
    nst, nz, full, deep = states.shape
    wide = full // peers
    rows = edge
    chunks = wide // rows
    steps = plan(chunks)
    f32 = jnp.float32
    dma = pltpu.SemaphoreType.DMA
    return pl.pallas_call(
        functools.partial(kernel, peers, slabs, rows, steps),
        out_shape=pltpu.VMEM((nz, wide, deep), f32),
        in_specs=[
            pl.BlockSpec(memory_space=pl.ANY),
            pl.BlockSpec(memory_space=pltpu.SMEM),
            pl.BlockSpec(memory_space=pl.ANY),
        ],
        out_specs=pl.BlockSpec(memory_space=pltpu.VMEM),
        scratch_shapes=[
            pltpu.VMEM((peers, nst, nz, wide, deep), f32),
            pltpu.VMEM((nz, wide, deep), f32),
            pltpu.VMEM((chunks, peers - 1, nz, rows, deep), f32),
            pltpu.VMEM((chunks, peers - 1, nz, rows, deep), f32),
            pltpu.VMEM((5 * nz, wide + 2 * edge, deep), f32),
            pltpu.VMEM((3 * nz, wide, deep), f32),
            pltpu.VMEM((nz, wide + 2 * edge, deep), f32),
            pltpu.VMEM((2, 2, nz, 2, deep), f32),
            pltpu.VMEM((2, 2, nz, 2, deep), f32),
            pltpu.VMEM((2, nz, 2, deep), f32),
            dma((peers,)),
            dma,
            dma((peers - 1, chunks)),
            dma((peers - 1, chunks)),
            dma((3, chunks)),
            dma((3, chunks)),
            dma((chunks,)),
            dma((chunks,)),
            dma((2, 2)),
            dma((2, 2)),
            dma,
            dma,
        ],
        compiler_params=pltpu.CompilerParams(
            collective_id=0, has_side_effects=True, vmem_limit_bytes=67043328 - 1024 * 1024
        ),
    )(states, occupations, core_density)


def solution(mesh):
    return jax.shard_map(
        functools.partial(shards, mesh.shape["interval"], mesh.shape["slab"]),
        mesh=mesh,
        in_specs=(P("interval", "slab", None, None), P("interval"), P("slab", None, None)),
        out_specs=P("slab", "interval", None),
        check_vma=False,
    )
```
